32 devices in a mesh: leaf: 2 (over core), row: 4 (over z), col: 4 (over y, x).
Axes of the slice: x: 2, y: 2, z: 4, core: 2. Of those that a mesh axis runs over, the one named last changes fastest.
Arguments:
- hidden_in: bfloat16 [10240, 2048], P(('leaf', 'row', 'col')), may hold values from -6 to 6
- per_layer_in: bfloat16 [10240, 256], P(('leaf', 'row', 'col')), may hold values from -6 to 6
- cotangent: bfloat16 [10240, 2048], P(('leaf', 'row', 'col')), may hold values from -6 to 6
- norm_in: float32 [2048], replicated, may hold values from 0.25 to 1.75
- w_query: bfloat16 [2048, 2048], P(None, 'row'), may hold values from -0.125 to 0.125
- w_key: bfloat16 [2048, 512], replicated, may hold values from -0.125 to 0.125
- w_value: bfloat16 [2048, 512], replicated, may hold values from -0.125 to 0.125
- query_norm: float32 [256], replicated, may hold values from 0.25 to 1.75
- key_norm: float32 [256], replicated, may hold values from 0.25 to 1.75
- w_out: bfloat16 [2048, 2048], P('row'), may hold values from -0.125 to 0.125
- post_attn_norm: float32 [2048], replicated, may hold values from 0.25 to 1.75
- laurel_left: bfloat16 [2048, 64], replicated, may hold values from -0.125 to 0.125
- laurel_right: bfloat16 [64, 2048], replicated, may hold values from -0.75 to 0.75
- laurel_norm: float32 [2048], replicated, may hold values from 0.25 to 1.75
- pre_ffn_norm: float32 [2048], replicated, may hold values from 0.25 to 1.75
- w_gate: bfloat16 [2048, 8192], P(None, 'row'), may hold values from -0.125 to 0.125
- w_up: bfloat16 [2048, 8192], P(None, 'row'), may hold values from -0.125 to 0.125
- w_down: bfloat16 [8192, 2048], P('row'), may hold values from -0.0625 to 0.0625
- post_ffn_norm: float32 [2048], replicated, may hold values from 0.25 to 1.75
- per_layer_gate: bfloat16 [2048, 256], replicated, may hold values from -0.125 to 0.125
- per_layer_proj: bfloat16 [256, 2048], replicated, may hold values from -0.375 to 0.375
- per_layer_norm: float32 [2048], replicated, may hold values from 0.25 to 1.75
- parents: int32 [26], replicated, may hold values from 0 to 25, as said below
- segment: int32 [10240], replicated, may hold values from 0 to 25, as said below
- position: int32 [10240], replicated, may hold values from 0 to 2559, as said below
Outputs:
- output: float32 [10240, 2048], P(('leaf', 'row', 'col'))
- input_grad: float32 [10240, 2048], P(('leaf', 'row', 'col'))
- per_layer_in_grad: float32 [10240, 256], P(('leaf', 'row', 'col'))
- norm_in_grad: float32 [2048], replicated
- w_query_grad: float32 [2048, 2048], P(('leaf', 'col'), 'row')
- w_key_grad: float32 [2048, 512], P(None, 'row')
- w_value_grad: float32 [2048, 512], P(None, 'row')
- query_norm_grad: float32 [256], replicated
- key_norm_grad: float32 [256], replicated
- w_out_grad: float32 [2048, 2048], P('row', ('leaf', 'col'))
- post_attn_norm_grad: float32 [2048], replicated
- laurel_left_grad: float32 [2048, 64], replicated
- laurel_right_grad: float32 [64, 2048], replicated
- laurel_norm_grad: float32 [2048], replicated
- pre_ffn_norm_grad: float32 [2048], replicated
- w_gate_grad: float32 [2048, 8192], P(('leaf', 'col'), 'row')
- w_up_grad: float32 [2048, 8192], P(('leaf', 'col'), 'row')
- w_down_grad: float32 [8192, 2048], P('row', ('leaf', 'col'))
- post_ffn_norm_grad: float32 [2048], replicated
- per_layer_gate_grad: float32 [2048, 256], replicated
- per_layer_proj_grad: float32 [256, 2048], replicated
- per_layer_norm_grad: float32 [2048], replicated
The draws below stay inside these ranges and needn't reach their ends.
Inputs may be any that keep to these rules, and one draw needn't show every extreme that they name: parents[s] is the segment that segment s continues: every tree has one trunk of 2048 tokens that names itself, four branches of 256 tokens that name the trunk, and eight leaves of 256 tokens, two on each branch, that name their branch; segment numbers are drawn at random. Reading the tokens of one leaf index in the order of col index, then row index, then a device's rows, each tree fills 5120 consecutive tokens, and the tokens of each segment lie together, segments in an order drawn for each tree. `position`: A token's place on its path: a trunk's tokens take 0 to 2047, a branch's start at 2048, a leaf's at 2304, rising by one within a segment.
All inputs are finite; a program needn't handle non-finite values.
Results may differ from the reference program's by a relative error of at most 0.022.
Values may be sent and summed in bfloat16 or wider, within the bound.
A program may use at most 384 MiB of HBM per device.

```python
import math
from functools import partial
import jax
import jax.numpy as jnp
from jax import lax

D = 2048
H = 8
KV = 2
HD = 256
FF = 8192
R = 64
P_SIZE = 256
TRUNK = 2048
BRANCH = 256
LEAF = 256
TREE_LEN = 5120
ROWS_DEV = 320
TOKENS = 10240
TREES = 2
N_LEAF = 2
N_ROW = 4
N_COL = 4


def tree_layout(key):
    tree_count = TOKENS // TREE_LEN
    seg_total = 13 * tree_count
    base_key = jax.random.fold_in(key, 7)
    middle = (jax.random.permutation(jax.random.fold_in(base_key, 1), seg_total - 2) + 1).astype(jnp.int32)
    ends = jnp.array([0, seg_total - 1], jnp.int32)
    ident = jnp.concatenate([ends, middle]).reshape(tree_count, 13)
    order_keys = jax.random.split(jax.random.fold_in(base_key, 2), tree_count)

    def one_order(order_key):
        return jax.random.permutation(order_key, 13)
    orders = jax.vmap(one_order)(order_keys).astype(jnp.int32)
    local_length = jnp.array([TRUNK] + [BRANCH] * 4 + [LEAF] * 8, jnp.int32)
    local_depth = jnp.array([0] + [TRUNK] * 4 + [TRUNK + BRANCH] * 8, jnp.int32)
    local_parent = jnp.array([0, 0, 0, 0, 0, 1, 1, 2, 2, 3, 3, 4, 4], jnp.int32)
    slot_length = local_length[orders]
    slot_end = jnp.cumsum(slot_length, axis=1)
    slot_start = slot_end - slot_length
    offsets = jnp.arange(TREE_LEN, dtype=jnp.int32)
    slot = jnp.sum((offsets[None, :, None] >= slot_end[:, None, :]).astype(jnp.int32), axis=2)
    local_seg = jnp.take_along_axis(orders, slot, axis=1)
    seg_start = jnp.take_along_axis(slot_start, slot, axis=1)
    seg_view = jnp.take_along_axis(ident, local_seg, axis=1)
    place_view = local_depth[local_seg] + offsets[None, :] - seg_start
    parent_table = jnp.zeros((seg_total,), jnp.int32).at[ident.reshape(-1)].set(ident[:, local_parent].reshape(-1))
    return (seg_view, place_view, parent_table)


def to_global(view_values):
    grid = view_values.reshape(N_LEAF, N_COL, N_ROW, ROWS_DEV)
    return jnp.transpose(grid, (0, 2, 1, 3)).reshape(TOKENS)


def draw_parents(key, part):
    seg_view, place_view, parent_table = tree_layout(key)
    return parent_table


def draw_segment(key, part):
    seg_view, place_view, parent_table = tree_layout(key)
    return to_global(seg_view)


def draw_position(key, part):
    seg_view, place_view, parent_table = tree_layout(key)
    return to_global(place_view)


def strengthened(result, key, source, target, blocks, factor):
    def block_of(axis_at):
        return (jnp.arange(result.shape[axis_at]) // (result.shape[axis_at] // blocks)).reshape((-1,) + (1,) * (result.ndim - 1 - axis_at))

    near = jax.random.permutation(key, blocks)[block_of(target)]
    other_side = (block_of(target) + blocks // 2) % blocks
    return jnp.where((block_of(source) == near) | (block_of(source) == other_side), factor * result, result)


def level_of(rng, extent, shards, smallest, high):
    loudness = 1.0
    for dim, shards_of in shards:
        heights = jax.random.uniform(jax.random.fold_in(jax.random.fold_in(rng, 6), dim), (shards_of,), jnp.float32, smallest / len(shards), high / len(shards))
        loudness = loudness * jnp.repeat(jnp.exp(heights), extent[dim] // shards_of).reshape((-1,) + (1,) * (len(extent) - 1 - dim))
    return loudness


def gaussian(key, dims, deviation, most, shards=(), held_as=jnp.bfloat16):
    values = deviation * jax.random.normal(key, dims, jnp.float32)
    if shards:
        values = values * level_of(key, dims, shards, -0.22, 0.18)
    return jnp.clip(values, -most, most).astype(held_as)


def bell_draw_with(key, extent, width, limit, cuts, heavy, held_as=jnp.bfloat16):
    entries = width * jax.random.normal(key, extent, jnp.float32)
    if cuts:
        entries = entries * level_of(key, extent, cuts, -0.22, 0.18)
    return jnp.clip(strengthened(entries, jax.random.fold_in(key, 3), *heavy), -limit, limit).astype(held_as)


def setup_inputs(seed: int = 0) -> dict:
    arg_keys = jax.random.split(jax.random.key(seed), 26)
    hidden_in = gaussian(arg_keys[0], (TOKENS, D), 1.0, 6.0, ((0, 32),))
    per_layer_in = gaussian(arg_keys[1], (TOKENS, P_SIZE), 1.0, 6.0, ((0, 32),))
    cotangent = bell_draw_with(arg_keys[2], (TOKENS, D), 1.0, 6.0, ((0, 32),), (0, 1, 32, 2.75))
    norm_in = jnp.clip(1.0 + 0.15 * jax.random.normal(arg_keys[3], (D,), jnp.float32), 0.25, 1.75)
    w_query = gaussian(arg_keys[4], (D, H * HD), D ** -0.5, 0.125, ((1, 4),))
    w_key = gaussian(arg_keys[5], (D, KV * HD), D ** -0.5, 0.125)
    w_value = gaussian(arg_keys[6], (D, KV * HD), D ** -0.5, 0.125)
    query_norm = jnp.clip(1.0 + 0.15 * jax.random.normal(arg_keys[7], (HD,), jnp.float32), 0.25, 1.75)
    key_norm = jnp.clip(1.0 + 0.15 * jax.random.normal(arg_keys[8], (HD,), jnp.float32), 0.25, 1.75)
    w_out = gaussian(arg_keys[9], (H * HD, D), (H * HD) ** -0.5, 0.125, ((0, 4),))
    post_attn_norm = jnp.clip(1.0 + 0.15 * jax.random.normal(arg_keys[10], (D,), jnp.float32), 0.25, 1.75)
    laurel_left = gaussian(arg_keys[11], (D, R), D ** -0.5, 0.125)
    laurel_right = gaussian(arg_keys[12], (R, D), R ** -0.5, 0.75)
    laurel_norm = jnp.clip(1.0 + 0.15 * jax.random.normal(arg_keys[13], (D,), jnp.float32), 0.25, 1.75)
    pre_ffn_norm = jnp.clip(1.0 + 0.15 * jax.random.normal(arg_keys[14], (D,), jnp.float32), 0.25, 1.75)
    w_gate = gaussian(arg_keys[15], (D, FF), D ** -0.5, 0.125, ((1, 4),))
    w_up = gaussian(arg_keys[16], (D, FF), D ** -0.5, 0.125, ((1, 4),))
    w_down = gaussian(arg_keys[17], (FF, D), FF ** -0.5, 0.0625, ((0, 4),))
    post_ffn_norm = jnp.clip(1.0 + 0.15 * jax.random.normal(arg_keys[18], (D,), jnp.float32), 0.25, 1.75)
    per_layer_gate = gaussian(arg_keys[19], (D, P_SIZE), D ** -0.5, 0.125)
    per_layer_proj = gaussian(arg_keys[20], (P_SIZE, D), P_SIZE ** -0.5, 0.375)
    per_layer_norm = jnp.clip(1.0 + 0.15 * jax.random.normal(arg_keys[21], (D,), jnp.float32), 0.25, 1.75)
    parents = draw_parents(jax.random.fold_in(arg_keys[25], 71), 0)
    segment = draw_segment(jax.random.fold_in(arg_keys[25], 71), 0)
    position = draw_position(jax.random.fold_in(arg_keys[25], 71), 0)
    return {"hidden_in": hidden_in, "per_layer_in": per_layer_in, "cotangent": cotangent, "norm_in": norm_in, "w_query": w_query, "w_key": w_key, "w_value": w_value, "query_norm": query_norm, "key_norm": key_norm, "w_out": w_out, "post_attn_norm": post_attn_norm, "laurel_left": laurel_left, "laurel_right": laurel_right, "laurel_norm": laurel_norm, "pre_ffn_norm": pre_ffn_norm, "w_gate": w_gate, "w_up": w_up, "w_down": w_down, "post_ffn_norm": post_ffn_norm, "per_layer_gate": per_layer_gate, "per_layer_proj": per_layer_proj, "per_layer_norm": per_layer_norm, "parents": parents, "segment": segment, "position": position}


EPS = 1e-06
ROPE_BASE = 1000000.0
INV_ROOT2 = 0.7071067811865476
HIGHEST = lax.Precision.HIGHEST

@jax.custom_vjp
def low(v):
    return lax.optimization_barrier(v.astype(jnp.bfloat16)).astype(jnp.float32)

@jax.custom_vjp
def low_back(v):
    return v

def low_keep(v):
    return (low(v), None)

def low_pass(kept, grad):
    return (grad,)

def back_keep(v):
    return (v, None)

def back_low(kept, grad):
    return (low(grad),)
low.defvjp(low_keep, low_pass)
low_back.defvjp(back_keep, back_low)

def matmul(left, right):
    return jnp.dot(left, right, precision=HIGHEST, preferred_element_type=jnp.float32)

def rms_norm(vector, gain):
    return vector * lax.rsqrt(lax.optimization_barrier(jnp.mean(vector * vector, axis=-1, keepdims=True)) + EPS) * gain

def rope_tables(places):
    index = jnp.arange(HD // 2).astype(jnp.float32)
    freq = jnp.exp(index * (-2.0 * math.log(ROPE_BASE) / HD))
    angle = places.astype(jnp.float32)[:, None] * freq[None, :]
    return (jnp.cos(angle)[:, None, :], jnp.sin(angle)[:, None, :])

def rotate(vector, angle_cos, angle_sin):
    half = vector.shape[-1] // 2
    first = vector[..., :half]
    second = vector[..., half:]
    return jnp.concatenate([first * angle_cos - second * angle_sin, second * angle_cos + first * angle_sin], axis=-1)

def to_view(values):
    rest = values.shape[1:]
    grid = values.reshape((N_LEAF, N_ROW, N_COL, ROWS_DEV) + rest)
    order = (0, 2, 1, 3) + tuple(range(4, 4 + len(rest)))
    return jnp.transpose(grid, order).reshape((TREES, TREE_LEN) + rest)

def from_view(values):
    rest = values.shape[2:]
    grid = values.reshape((N_LEAF, N_COL, N_ROW, ROWS_DEV) + rest)
    order = (0, 2, 1, 3) + tuple(range(4, 4 + len(rest)))
    return jnp.transpose(grid, order).reshape((TOKENS,) + rest)

def attend_tree(query_low, key_low, value_low, seg_ids, place_ids, first_up, second_up):
    visible = ((seg_ids[None, :] == seg_ids[:, None]) | (seg_ids[None, :] == first_up[:, None]) | (seg_ids[None, :] == second_up[:, None])) & (place_ids[None, :] <= place_ids[:, None])
    group_size = H // KV
    key_heads = jnp.repeat(key_low, group_size, axis=1)
    value_heads = jnp.repeat(value_low, group_size, axis=1)
    score_scale = HD ** (-0.5)

    def head_fn(item):
        query_head, key_head, value_head = item
        scores = low_back(jnp.dot(query_head, key_head.T, precision=HIGHEST) * score_scale)
        scores = jnp.where(visible, scores, -1e+30)
        row_top = lax.optimization_barrier(jnp.max(scores, axis=1, keepdims=True))
        weights = jnp.exp(scores - row_top)
        weights = weights / lax.optimization_barrier(jnp.sum(weights, axis=1, keepdims=True))
        return jnp.dot(low(weights), value_head, precision=HIGHEST)
    outputs = lax.map(jax.checkpoint(head_fn), (jnp.swapaxes(query_low, 0, 1), jnp.swapaxes(key_heads, 0, 1), jnp.swapaxes(value_heads, 0, 1)))
    return jnp.swapaxes(outputs, 0, 1)

def attention(query_low, key_low, value_low, seg_ids, place_ids, first_up, second_up):

    def tree_step(carry, item):
        return (carry, attend_tree(*item))
    items = (to_view(query_low), to_view(key_low), to_view(value_low), to_view(seg_ids), to_view(place_ids), to_view(first_up), to_view(second_up))
    _, outputs = lax.scan(jax.checkpoint(tree_step), None, items)
    return from_view(outputs)

def gelu_tanh(vector):
    return jax.nn.gelu(vector, approximate=True)

def layer(ints, stream_in, side_input, norm_in, w_query, w_key, w_value, query_norm, key_norm, w_out, post_attn_norm, laurel_left, laurel_right, laurel_norm, pre_ffn_norm, w_gate, w_up, w_down, post_ffn_norm, per_layer_gate, per_layer_proj, per_layer_norm):
    seg_ids, place_ids, first_up, second_up = ints
    angle_cos, angle_sin = rope_tables(place_ids)
    normed = rms_norm(stream_in, norm_in)
    normed_low = low(normed)
    query_raw = low_back(matmul(normed_low, w_query)).reshape(TOKENS, H, HD)
    key_raw = low_back(matmul(normed_low, w_key)).reshape(TOKENS, KV, HD)
    value_raw = low_back(matmul(normed_low, w_value)).reshape(TOKENS, KV, HD)
    query_low = low(rotate(rms_norm(query_raw, query_norm), angle_cos, angle_sin))
    key_low = low(rotate(rms_norm(key_raw, key_norm), angle_cos, angle_sin))
    value_low = low(value_raw)
    attended = attention(query_low, key_low, value_low, seg_ids, place_ids, first_up, second_up)
    attended_low = low(low_back(attended)).reshape(TOKENS, H * HD)
    attn_raw = low_back(matmul(attended_low, w_out))
    laurel_mid = low(low_back(matmul(normed_low, laurel_left)))
    laurel_raw = low_back(matmul(laurel_mid, laurel_right))
    stream_one = (stream_in + rms_norm(attn_raw, post_attn_norm) + normed + rms_norm(laurel_raw, laurel_norm)) * INV_ROOT2
    ffn_input = low(rms_norm(stream_one, pre_ffn_norm))
    gate_value = low_back(matmul(ffn_input, w_gate))
    up_value = low_back(matmul(ffn_input, w_up))
    hidden = low(gelu_tanh(gate_value) * up_value)
    ffn_raw = low_back(matmul(hidden, w_down))
    stream_two = stream_one + rms_norm(ffn_raw, post_ffn_norm)
    side_pre = low_back(matmul(low(stream_two), per_layer_gate))
    side_mid = low(gelu_tanh(side_pre) * side_input)
    side_raw = low_back(matmul(side_mid, per_layer_proj))
    return stream_two + rms_norm(side_raw, per_layer_norm)

def reference(hidden_in, per_layer_in, cotangent, norm_in, w_query, w_key, w_value, query_norm, key_norm, w_out, post_attn_norm, laurel_left, laurel_right, laurel_norm, pre_ffn_norm, w_gate, w_up, w_down, post_ffn_norm, per_layer_gate, per_layer_proj, per_layer_norm, parents, segment, position):
    first_up = parents[segment]
    second_up = parents[first_up]
    floats = (hidden_in.astype(jnp.float32), per_layer_in.astype(jnp.float32), norm_in.astype(jnp.float32), w_query.astype(jnp.float32), w_key.astype(jnp.float32), w_value.astype(jnp.float32), query_norm.astype(jnp.float32), key_norm.astype(jnp.float32), w_out.astype(jnp.float32), post_attn_norm.astype(jnp.float32), laurel_left.astype(jnp.float32), laurel_right.astype(jnp.float32), laurel_norm.astype(jnp.float32), pre_ffn_norm.astype(jnp.float32), w_gate.astype(jnp.float32), w_up.astype(jnp.float32), w_down.astype(jnp.float32), post_ffn_norm.astype(jnp.float32), per_layer_gate.astype(jnp.float32), per_layer_proj.astype(jnp.float32), per_layer_norm.astype(jnp.float32))
    output, pull = jax.vjp(partial(layer, (segment, position, first_up, second_up)), *floats)
    grads = pull(cotangent.astype(jnp.float32))
    return (output, grads[0], grads[1], grads[2], grads[3], grads[4], grads[5], grads[6], grads[7], grads[8], grads[9], grads[10], grads[11], grads[12], grads[13], grads[14], grads[15], grads[16], grads[17], grads[18], grads[19], grads[20])
```

```python
import functools
import math

import jax
import jax.numpy as jnp
from jax import lax
from jax.experimental import pallas as pl
from jax.experimental.pallas import tpu as pltpu
from jax.sharding import PartitionSpec as P

H = 8
KV = 2
HD = 256
TRUNK = 2048
BRANCH = 256
LEAF = 256
KEY_BLOCK = 256
GROUP = H // KV
LOG2E = 1.4426950408889634


EPS = 1e-06
ROPE_BASE = 1000000.0
INV_ROOT2 = 0.7071067811865476


def product(left, right):
    return jnp.dot(left, right, preferred_element_type=jnp.float32)


def product_nt(left, right):
    return lax.dot_general(
        left, right, (((1,), (1,)), ((), ())), preferred_element_type=jnp.float32
    )


def product_tn(left, right):
    return lax.dot_general(
        left, right, (((0,), (0,)), ((), ())), preferred_element_type=jnp.float32
    )


def rms_norm(vector, gain):
    return vector * lax.rsqrt(jnp.mean(vector * vector, axis=-1, keepdims=True) + EPS) * gain


def gelu_tanh(vector):
    return jax.nn.gelu(vector, approximate=True)


def rope_tables(places):
    index = jnp.arange(HD // 2, dtype=jnp.float32)
    freq = jnp.exp(index * (-2.0 * math.log(ROPE_BASE) / HD))
    angle = places.astype(jnp.float32)[:, None] * freq[None, :]
    return (jnp.cos(angle)[:, None, :], jnp.sin(angle)[:, None, :])


def rotate(vector, angle_cos, angle_sin):
    half = vector.shape[-1] // 2
    first = vector[..., :half]
    second = vector[..., half:]
    return jnp.concatenate(
        [first * angle_cos - second * angle_sin, second * angle_cos + first * angle_sin], axis=-1
    )


def head_prep(raw, gain, angle_cos, angle_sin):
    heads = raw.reshape(raw.shape[0], -1, gain.shape[0])
    return rotate(rms_norm(heads, gain), angle_cos, angle_sin)


def head_rows(ref, kv_head, head_width):
    base = kv_head * GROUP * head_width
    return jnp.concatenate(
        [ref[:, base + g * head_width : base + (g + 1) * head_width] for g in range(GROUP)], axis=0
    )


def attend_kernel(scale, key_heads, idx, count, own, offset, q_ref, kv_ref, o_ref, lse_ref, acc, den):
    step = pl.program_id(0)
    sub = q_ref.shape[0]
    width = q_ref.shape[1] // (key_heads * GROUP)
    rows = GROUP * sub
    queries = [head_rows(q_ref, h, width) for h in range(key_heads)]

    def block(start, mask):
        for h in range(key_heads):
            keys = kv_ref[pl.ds(start, KEY_BLOCK), h * width : (h + 1) * width]
            values = kv_ref[pl.ds(start, KEY_BLOCK), (key_heads + h) * width : (key_heads + h + 1) * width]
            weights = jnp.exp2(product_nt(queries[h], keys) * (scale * LOG2E))
            if mask is not None:
                weights = jnp.where(mask, weights, 0.0)
            part = product(weights.astype(jnp.bfloat16), values)
            if mask is not None:
                acc[h] = part
                den[h] = weights
            else:
                acc[h] += part
                den[h] += weights

    token = offset[step] + lax.broadcasted_iota(jnp.int32, (rows, KEY_BLOCK), 0) % sub
    place = lax.broadcasted_iota(jnp.int32, (rows, KEY_BLOCK), 1)
    block(pl.multiple_of(own[step] * KEY_BLOCK, KEY_BLOCK), place <= token)

    def body(j, carry):
        block(pl.multiple_of(idx[step, j] * KEY_BLOCK, KEY_BLOCK), None)
        return carry

    lax.fori_loop(0, count[step], body, 0)
    for h in range(key_heads):
        total = jnp.sum(den[h], axis=1, keepdims=True)
        result = (acc[h] / total).astype(jnp.bfloat16)
        for g in range(GROUP):
            at = (h * GROUP + g) * width
            o_ref[:, at : at + width] = result[g * sub : (g + 1) * sub]
        lse_ref[0, h] = jnp.transpose(jnp.broadcast_to(jnp.log2(total), (rows, 128)))[:8]


def attend_back_kernel(
    scale, key_heads, idx, count, own, offset, q_ref, d_ref, lse_ref, mid_ref, kv_ref, dq_ref, dkv_ref, acc, dq
):
    step = pl.program_id(0)
    sub = q_ref.shape[0]
    width = q_ref.shape[1] // (key_heads * GROUP)
    rows = GROUP * sub
    queries = [head_rows(q_ref, h, width) for h in range(key_heads)]
    grads = [head_rows(d_ref, h, width) for h in range(key_heads)]

    @pl.when(step == 0)
    def _():
        acc[...] = jnp.zeros_like(acc)

    def block(start, mask):
        for h in range(key_heads):
            k_at = slice(h * width, (h + 1) * width)
            v_at = slice((key_heads + h) * width, (key_heads + h + 1) * width)
            keys = kv_ref[pl.ds(start, KEY_BLOCK), k_at]
            values = kv_ref[pl.ds(start, KEY_BLOCK), v_at]
            weights = jnp.exp2(product_nt(keys, queries[h]) * (scale * LOG2E) - lse_ref[0, h, :1])
            if mask is not None:
                weights = jnp.where(mask, weights, 0.0)
            slopes = (weights * (product_nt(values, grads[h]) - mid_ref[0, h, :1])).astype(jnp.bfloat16)
            acc[pl.ds(start, KEY_BLOCK), v_at] += product(weights.astype(jnp.bfloat16), grads[h])
            acc[pl.ds(start, KEY_BLOCK), k_at] += product(slopes, queries[h])
            part = product_tn(slopes, keys)
            if mask is not None:
                dq[h] = part
            else:
                dq[h] += part

    token = offset[step] + lax.broadcasted_iota(jnp.int32, (KEY_BLOCK, rows), 1) % sub
    place = lax.broadcasted_iota(jnp.int32, (KEY_BLOCK, rows), 0)
    block(pl.multiple_of(own[step] * KEY_BLOCK, KEY_BLOCK), place <= token)

    def body(j, carry):
        block(pl.multiple_of(idx[step, j] * KEY_BLOCK, KEY_BLOCK), None)
        return carry

    lax.fori_loop(0, count[step], body, 0)
    for h in range(key_heads):
        for g in range(GROUP):
            at = (h * GROUP + g) * width
            dq_ref[:, at : at + width] = dq[h, g * sub : (g + 1) * sub] * scale

    @pl.when(step == pl.num_programs(0) - 1)
    def _():
        half = key_heads * width

        def out(j, carry):
            at = pl.ds(pl.multiple_of(j * KEY_BLOCK, KEY_BLOCK), KEY_BLOCK)
            dkv_ref[at, :half] = (acc[at, :half] * scale).astype(jnp.bfloat16)
            dkv_ref[at, half:] = acc[at, half:].astype(jnp.bfloat16)
            return carry

        lax.fori_loop(0, acc.shape[0] // KEY_BLOCK, out, 0)


def attend(plan, query_b, kv_tree, sub):
    tokens, total = query_b.shape
    key_heads = KV
    width = total // H
    steps = tokens // sub
    rows = GROUP * sub
    return pl.pallas_call(
        functools.partial(attend_kernel, width ** (-0.5), key_heads),
        out_shape=(
            jax.ShapeDtypeStruct((tokens, total), jnp.bfloat16),
            jax.ShapeDtypeStruct((steps, key_heads, 8, rows), jnp.float32),
        ),
        grid_spec=pltpu.PrefetchScalarGridSpec(
            num_scalar_prefetch=4,
            grid=(steps,),
            in_specs=[
                pl.BlockSpec((sub, total), lambda i, *_: (i, 0)),
                pl.BlockSpec(kv_tree.shape, lambda i, *_: (0, 0), pipeline_mode=pl.Buffered(1)),
            ],
            out_specs=[
                pl.BlockSpec((sub, total), lambda i, *_: (i, 0)),
                pl.BlockSpec((1, key_heads, 8, rows), lambda i, *_: (i, 0, 0, 0)),
            ],
            scratch_shapes=[
                pltpu.VMEM((key_heads, rows, width), jnp.float32),
                pltpu.VMEM((key_heads, rows, KEY_BLOCK), jnp.float32),
            ],
        ),
        compiler_params=pltpu.CompilerParams(vmem_limit_bytes=48 * 1024 * 1024),
        name="attend",
    )(*plan, query_b, kv_tree)


def attend_back(plan, query_b, grad_b, lse, middle, kv_tree, sub):
    tokens, total = query_b.shape
    key_heads = KV
    width = total // H
    steps = tokens // sub
    rows = GROUP * sub
    return pl.pallas_call(
        functools.partial(attend_back_kernel, width ** (-0.5), key_heads),
        out_shape=(
            jax.ShapeDtypeStruct((tokens, total), jnp.float32),
            jax.ShapeDtypeStruct(kv_tree.shape, jnp.bfloat16),
        ),
        grid_spec=pltpu.PrefetchScalarGridSpec(
            num_scalar_prefetch=4,
            grid=(steps,),
            in_specs=[
                pl.BlockSpec((sub, total), lambda i, *_: (i, 0)),
                pl.BlockSpec((sub, total), lambda i, *_: (i, 0)),
                pl.BlockSpec((1, key_heads, 8, rows), lambda i, *_: (i, 0, 0, 0)),
                pl.BlockSpec((1, key_heads, 1, rows), lambda i, *_: (i, 0, 0, 0)),
                pl.BlockSpec(kv_tree.shape, lambda i, *_: (0, 0), pipeline_mode=pl.Buffered(1)),
            ],
            out_specs=[
                pl.BlockSpec((sub, total), lambda i, *_: (i, 0)),
                pl.BlockSpec(kv_tree.shape, lambda i, *_: (0, 0), pipeline_mode=pl.Buffered(1)),
            ],
            scratch_shapes=[
                pltpu.VMEM(kv_tree.shape, jnp.float32),
                pltpu.VMEM((key_heads, rows, width), jnp.float32),
            ],
        ),
        compiler_params=pltpu.CompilerParams(vmem_limit_bytes=60 * 1024 * 1024),
        name="attend_back",
    )(*plan, query_b, grad_b, lse, middle, kv_tree)


def key_plan(parents, segment, position, rows, view_start, tree_start, tree_length, sub, leaf, sizes):
    leaf_devices, row_devices, col_devices = sizes

    def blocks(values):
        grid = values.reshape(leaf_devices, row_devices, col_devices, rows)
        mine = lax.dynamic_index_in_dim(grid, leaf, 0, keepdims=False)
        view = jnp.transpose(mine, (1, 0, 2)).reshape(-1, KEY_BLOCK)[:, 0]
        return lax.dynamic_slice_in_dim(view, tree_start // KEY_BLOCK, tree_length // KEY_BLOCK)

    def pick(table, index):
        at = jnp.arange(table.shape[0], dtype=jnp.int32)
        return jnp.sum(jnp.where(index[:, None] == at[None, :], table[None, :], 0), axis=1)

    block_segment = blocks(segment)
    block_place = blocks(position)
    begin = view_start - tree_start + sub * jnp.arange(rows // sub, dtype=jnp.int32)
    own = begin // KEY_BLOCK
    offset = begin % KEY_BLOCK
    query_segment = pick(block_segment, own)
    query_place = pick(block_place, own) + offset
    first = pick(parents, query_segment)
    second = pick(parents, first)
    number = jnp.arange(tree_length // KEY_BLOCK, dtype=jnp.int32)
    seen = (
        (block_segment[None, :] == query_segment[:, None])
        | (block_segment[None, :] == first[:, None])
        | (block_segment[None, :] == second[:, None])
    )
    seen = seen & (block_place[None, :] <= query_place[:, None]) & (number[None, :] != own[:, None])
    flags = seen.astype(jnp.int32)
    before = number[:, None] < number[None, :]
    rank = jnp.sum(jnp.where(before[None], flags[:, :, None], 0), axis=1)
    slot = (rank[:, None, :] == number[None, :, None]) & seen[:, None, :]
    idx = jnp.sum(jnp.where(slot, number[None, None, :], 0), axis=2)
    return idx, jnp.sum(flags, axis=1), own, offset


def per_device(
    hidden_in,
    per_layer_in,
    cotangent,
    norm_in,
    w_query,
    w_key,
    w_value,
    query_norm,
    key_norm,
    w_out,
    post_attn_norm,
    laurel_left,
    laurel_right,
    laurel_norm,
    pre_ffn_norm,
    w_gate,
    w_up,
    w_down,
    post_ffn_norm,
    per_layer_gate,
    per_layer_proj,
    per_layer_norm,
    parents,
    segment,
    position,
):
    bf16 = jnp.bfloat16
    row_count = hidden_in.shape[0]
    head_width = query_norm.shape[0]
    row_devices = lax.axis_size("row")
    col_devices = lax.axis_size("col")
    leaf_index = lax.axis_index("leaf")
    row_index = lax.axis_index("row")
    col_index = lax.axis_index("col")
    block_rows = row_count * row_devices
    group_rows = block_rows * col_devices
    tree_length = TRUNK + 4 * BRANCH + 8 * LEAF
    leaf_devices = lax.axis_size("leaf")
    key_width = w_key.shape[1]
    key_heads = key_width // head_width
    view_start = (col_index * row_devices + row_index) * row_count
    tree_start = view_start // tree_length * tree_length
    sub = math.gcd(row_count, KEY_BLOCK)
    own_place = lax.dynamic_slice_in_dim(
        position,
        ((leaf_index * row_devices + row_index) * col_devices + col_index) * row_count,
        row_count,
    )
    plan = key_plan(
        parents,
        segment,
        position,
        row_count,
        view_start,
        tree_start,
        tree_length,
        sub,
        leaf_index,
        (leaf_devices, row_devices, col_devices),
    )
    spread = leaf_devices * col_devices
    spot = leaf_index * col_devices + col_index
    stream_in = hidden_in.astype(jnp.float32)
    normed, in_back = jax.vjp(rms_norm, stream_in, norm_in)
    normed_b = normed.astype(bf16)
    own_cos, own_sin = rope_tables(own_place)

    def prep_fn(raw, gain):
        return head_prep(raw, gain, own_cos, own_sin)

    key_raw = product(normed_b, w_key)
    value_raw = product(normed_b, w_value)
    key_prep, key_back = jax.vjp(prep_fn, key_raw, key_norm)
    kv_own = jnp.concatenate([key_prep.reshape(row_count, key_width), value_raw], axis=1).astype(bf16)
    kv_block = lax.all_gather(kv_own, "row", axis=0, tiled=True)
    kv_tree = lax.all_gather(kv_block, "col", axis=0, tiled=True)
    if group_rows != tree_length:
        kv_tree = lax.dynamic_slice_in_dim(kv_tree, tree_start, tree_length, 0)
    query_part = w_query.shape[0] // spread
    w_query_piece = lax.dynamic_slice_in_dim(w_query, spot * query_part, query_part, 0)
    w_query_piece = lax.all_gather(w_query_piece, "row", axis=1, tiled=True)
    w_query_all = lax.all_gather(w_query_piece, ("leaf", "col"), axis=0, tiled=True)
    out_part = w_out.shape[0] // spread
    w_out_piece = lax.dynamic_slice_in_dim(w_out, spot * out_part, out_part, 0)
    w_out_piece = lax.all_gather(w_out_piece, "row", axis=0)
    w_out_all = lax.all_gather(w_out_piece, ("leaf", "col"), axis=1)
    w_out_all = w_out_all.reshape(w_query_all.shape[1], w_out.shape[1])
    query_raw = product(normed_b, w_query_all)
    query_prep, query_back = jax.vjp(prep_fn, query_raw, query_norm)
    query_b = query_prep.astype(bf16).reshape(row_count, -1)
    attended_b, lse = attend(plan, query_b, kv_tree, sub)
    attn_raw = product(attended_b, w_out_all)
    laurel_mid_b = product(normed_b, laurel_left).astype(bf16)
    laurel_raw = product(laurel_mid_b, laurel_right)

    def mix_one(stream_zero, attn_part, normed_part, laurel_part, attn_gain, laurel_gain):
        return (
            stream_zero
            + rms_norm(attn_part, attn_gain)
            + normed_part
            + rms_norm(laurel_part, laurel_gain)
        ) * INV_ROOT2

    stream_one, mix_back = jax.vjp(
        mix_one, stream_in, attn_raw, normed, laurel_raw, post_attn_norm, laurel_norm
    )
    ffn_input, ffn_in_back = jax.vjp(rms_norm, stream_one, pre_ffn_norm)
    ffn_input_b = ffn_input.astype(bf16)
    ffn_gathered = lax.all_gather(ffn_input_b, "row", axis=0, tiled=True)
    gate_value = product(ffn_gathered, w_gate)
    up_value = product(ffn_gathered, w_up)
    gelu_gate, gelu_back = jax.vjp(gelu_tanh, gate_value)
    hidden_b = (gelu_gate * up_value).astype(bf16)
    ffn_raw = lax.psum_scatter(
        product(hidden_b, w_down).astype(bf16), "row", scatter_dimension=0, tiled=True
    ).astype(jnp.float32)

    def mix_two(stream_part, ffn_part, ffn_gain):
        return stream_part + rms_norm(ffn_part, ffn_gain)

    stream_two, two_back = jax.vjp(mix_two, stream_one, ffn_raw, post_ffn_norm)
    stream_two_b = stream_two.astype(bf16)
    side_pre = product(stream_two_b, per_layer_gate)
    side_input = per_layer_in.astype(jnp.float32)
    side_act, side_act_back = jax.vjp(gelu_tanh, side_pre)
    side_b = (side_act * side_input).astype(bf16)
    side_raw = product(side_b, per_layer_proj)

    def mix_three(stream_part, side_part, side_gain):
        return stream_part + rms_norm(side_part, side_gain)

    output, three_back = jax.vjp(mix_three, stream_two, side_raw, per_layer_norm)
    grad_out = cotangent.astype(jnp.float32)
    grad_two, grad_side_raw, per_layer_norm_grad = three_back(grad_out)
    grad_side_b = grad_side_raw.astype(bf16)
    per_layer_proj_grad = product_tn(side_b, grad_side_b)
    grad_side = product_nt(grad_side_b, per_layer_proj)
    per_layer_in_grad = grad_side * side_act
    grad_pre_b = side_act_back(grad_side * side_input)[0].astype(bf16)
    per_layer_gate_grad = product_tn(stream_two_b, grad_pre_b)
    grad_two = grad_two + product_nt(grad_pre_b, per_layer_gate)
    grad_one, grad_ffn_raw, post_ffn_norm_grad = two_back(grad_two)
    grad_ffn_b = grad_ffn_raw.astype(bf16)
    grad_ffn_rows = lax.all_gather(grad_ffn_b, "row", axis=0, tiled=True)
    grad_hidden = product_nt(grad_ffn_rows, w_down)
    w_down_grad = product_tn(hidden_b, grad_ffn_rows)
    grad_gate_b = gelu_back(grad_hidden * up_value)[0].astype(bf16)
    grad_up_b = (grad_hidden * gelu_gate).astype(bf16)
    w_gate_grad = product_tn(ffn_gathered, grad_gate_b)
    w_up_grad = product_tn(ffn_gathered, grad_up_b)
    grad_ffn_input = lax.psum_scatter(
        (product_nt(grad_gate_b, w_gate) + product_nt(grad_up_b, w_up)).astype(jnp.bfloat16),
        "row",
        scatter_dimension=0,
        tiled=True,
    ).astype(jnp.float32)
    grad_one_extra, pre_ffn_norm_grad = ffn_in_back(grad_ffn_input)
    grad_one = grad_one + grad_one_extra
    (
        grad_zero,
        grad_attn_raw,
        grad_normed,
        grad_laurel_raw,
        post_attn_norm_grad,
        laurel_norm_grad,
    ) = mix_back(grad_one)
    grad_laurel_b = grad_laurel_raw.astype(bf16)
    laurel_right_grad = product_tn(laurel_mid_b, grad_laurel_b)
    grad_mid_b = product_nt(grad_laurel_b, laurel_right).astype(bf16)
    laurel_left_grad = product_tn(normed_b, grad_mid_b)
    grad_normed = grad_normed + product_nt(grad_mid_b, laurel_left)
    grad_attn_b = grad_attn_raw.astype(bf16)
    grad_vec_b = product_nt(grad_attn_b, w_out_all).astype(bf16)
    w_out_grad = product_tn(attended_b, grad_attn_b).astype(bf16)
    middle = jnp.sum(
        (grad_vec_b.astype(jnp.float32) * attended_b.astype(jnp.float32)).reshape(
            row_count, H, head_width
        ),
        axis=2,
    )
    middle = middle.reshape(row_count // sub, sub, key_heads, H // key_heads)
    middle = jnp.transpose(middle, (0, 2, 3, 1)).reshape(row_count // sub, key_heads, 1, -1)
    grad_query, grad_kv = attend_back(plan, query_b, grad_vec_b, lse, middle, kv_tree, sub)
    grad_query_raw, query_norm_grad = query_back(
        grad_query.reshape(row_count, H, head_width)
    )
    grad_query_b = grad_query_raw.astype(bf16)
    w_query_grad = product_tn(normed_b, grad_query_b).astype(bf16)
    if group_rows != tree_length:
        grad_kv = lax.dynamic_update_slice(
            jnp.zeros((group_rows, 2 * key_width), bf16), grad_kv, (tree_start, 0)
        )
    grad_kv = lax.psum_scatter(grad_kv, "col", scatter_dimension=0, tiled=True)
    grad_kv = lax.psum_scatter(grad_kv, "row", scatter_dimension=0, tiled=True)
    grad_value_b = grad_kv[:, key_width:]
    grad_key_raw, key_norm_grad = key_back(
        grad_kv[:, :key_width].astype(jnp.float32).reshape(row_count, key_heads, head_width)
    )
    grad_key_b = grad_key_raw.astype(bf16)
    w_key_full = product_tn(normed_b, grad_key_b)
    w_value_full = product_tn(normed_b, grad_value_b)
    grad_normed = (
        grad_normed
        + product_nt(grad_query_b, w_query_all)
        + product_nt(grad_key_b, w_key)
        + product_nt(grad_value_b, w_value)
    )
    grad_in_norm, norm_in_grad = in_back(grad_normed)
    input_grad = grad_zero + grad_in_norm
    both = ("leaf", "col")
    down_shard = lax.psum_scatter(w_down_grad.astype(bf16), both, scatter_dimension=1, tiled=True)
    gate_shard = lax.psum_scatter(w_gate_grad.astype(bf16), both, scatter_dimension=0, tiled=True)
    up_shard = lax.psum_scatter(w_up_grad.astype(bf16), both, scatter_dimension=0, tiled=True)
    out_shard = lax.psum_scatter(w_out_grad, both, scatter_dimension=1, tiled=True)
    out_shard = lax.psum_scatter(out_shard, "row", scatter_dimension=0, tiled=True)
    query_shard = lax.psum_scatter(w_query_grad, both, scatter_dimension=0, tiled=True)
    query_shard = lax.psum_scatter(query_shard, "row", scatter_dimension=1, tiled=True)
    down_shard, gate_shard, up_shard, out_shard, query_shard = (
        shard.astype(jnp.float32)
        for shard in (down_shard, gate_shard, up_shard, out_shard, query_shard)
    )
    every = ("leaf", "row", "col")
    quarter = key_width // row_devices
    pair = jnp.stack(
        [part.reshape(-1, row_devices, quarter) for part in (w_key_full, w_value_full)], axis=2
    )
    pair = jnp.transpose(pair, (1, 0, 2, 3)).reshape(row_devices, -1, 2 * quarter).astype(bf16)
    pair = lax.psum_scatter(pair, "row", scatter_dimension=0, tiled=True)[0]
    pair = lax.psum(pair.astype(jnp.float32), both)
    key_grad_part = pair[:, :quarter]
    value_grad_part = pair[:, quarter:]
    early = lax.psum(
        (
            laurel_left_grad,
            laurel_right_grad,
            per_layer_gate_grad,
            per_layer_proj_grad,
        ),
        every,
    )
    late = lax.psum(
        (
            norm_in_grad,
            query_norm_grad,
            key_norm_grad,
            post_attn_norm_grad,
            laurel_norm_grad,
            pre_ffn_norm_grad,
            post_ffn_norm_grad,
            per_layer_norm_grad,
        ),
        every,
    )
    return (
        output,
        input_grad,
        per_layer_in_grad,
        late[0],
        query_shard,
        key_grad_part,
        value_grad_part,
        late[1],
        late[2],
        out_shard,
        late[3],
        early[0],
        early[1],
        late[4],
        late[5],
        gate_shard,
        up_shard,
        down_shard,
        late[6],
        early[2],
        early[3],
        late[7],
    )


def solution(mesh):
    in_specs = (
        P(("leaf", "row", "col"), None),
        P(("leaf", "row", "col"), None),
        P(("leaf", "row", "col"), None),
        P(),
        P(None, "row"),
        P(),
        P(),
        P(),
        P(),
        P("row", None),
        P(),
        P(),
        P(),
        P(),
        P(),
        P(None, "row"),
        P(None, "row"),
        P("row", None),
        P(),
        P(),
        P(),
        P(),
        P(),
        P(),
        P(),
    )
    out_specs = (
        P(("leaf", "row", "col"), None),
        P(("leaf", "row", "col"), None),
        P(("leaf", "row", "col"), None),
        P(),
        P(("leaf", "col"), "row"),
        P(None, "row"),
        P(None, "row"),
        P(),
        P(),
        P("row", ("leaf", "col")),
        P(),
        P(),
        P(),
        P(),
        P(),
        P(("leaf", "col"), "row"),
        P(("leaf", "col"), "row"),
        P("row", ("leaf", "col")),
        P(),
        P(),
        P(),
        P(),
    )
    return jax.shard_map(
        per_device, mesh=mesh, in_specs=in_specs, out_specs=out_specs, check_vma=False
    )
```
